512 devices in a mesh: head: 16 (over z), span: 32 (over x, y, core).
Axes of the slice: x: 4, y: 4, z: 16, core: 2. Of those that a mesh axis runs over, the one named last changes fastest.
Arguments:
- queries: bfloat16 [65536, 2048], P(('span', 'head')), may hold values from -6 to 6
- keys: bfloat16 [65536, 2048], P(('span', 'head')), may hold values from -6 to 6
- values: bfloat16 [65536, 2048], P(('span', 'head')), may hold values from -6 to 6
- out_grad: bfloat16 [65536, 2048], P(('span', 'head')), may hold values from -6 to 6
Outputs:
- attn_out: bfloat16 [65536, 2048], P(('span', 'head'))
- query_gradient: bfloat16 [65536, 2048], P(('span', 'head'))
- grad_key: bfloat16 [65536, 2048], P(('span', 'head'))
- grad_value: bfloat16 [65536, 2048], P(('span', 'head'))
The draws below stay inside these ranges and needn't reach their ends.
All inputs are finite; a program needn't handle non-finite values.
Results may differ from the reference program's by a relative error of at most 0.0058.
Values may be sent and summed in bfloat16 or wider, within the bound.
A program may use at most 64 MiB of HBM per device.

```python
import jax
import jax.numpy as jnp
from jax import lax

HEADS = 16
DH = 128
BLK = 2048
SEQ = 65536
FEAT = 2048


def levels(stream_key, shape, shards, smallest, top_value):
    level = 1.0
    for dim, shards_of in shards:
        heights = jax.random.uniform(jax.random.fold_in(jax.random.fold_in(stream_key, 6), dim), (shards_of,), jnp.float32, smallest / len(shards), top_value / len(shards))
        level = level * jnp.repeat(jnp.exp(heights), shape[dim] // shards_of).reshape((-1,) + (1,) * (len(shape) - 1 - dim))
    return level


def scatter_about(stream_key, extent, deviation, limit, cuts=(), kind=jnp.bfloat16):
    drawn = deviation * jax.random.normal(stream_key, extent, jnp.float32)
    if cuts:
        drawn = drawn * levels(stream_key, extent, cuts, -0.22, 0.18)
    return jnp.clip(drawn, -limit, limit).astype(kind)


def setup_inputs(seed: int = 0) -> dict:
    splits = jax.random.split(jax.random.key(seed), 5)
    return {
        "queries": scatter_about(splits[0], (SEQ, FEAT), 1.0, 6.0, ((0, 512),)),
        "keys": scatter_about(splits[1], (SEQ, FEAT), 1.0, 6.0, ((0, 512),)),
        "values": scatter_about(splits[2], (SEQ, FEAT), 1.0, 6.0, ((0, 512),)),
        "out_grad": scatter_about(splits[3], (SEQ, FEAT), 1.0, 6.0, ((0, 512),)),
    }


def block_states(items):
    key_tile, value_tile, query_block, scaled_block = items
    forward_every = jnp.einsum('xgy,xgi->gyi', key_tile.astype(jnp.float32), value_tile.astype(jnp.float32))
    back_each = jnp.einsum('tnv,tnk->nvk', scaled_block.astype(jnp.float32), query_block.astype(jnp.float32))
    return (forward_every, back_each)

def block_terms(items):
    query_block, key_tile, value_tile, scaled_block, forward_narrow, back_low, scale_block = items
    token_count = query_block.shape[0]
    causal = jnp.tril(jnp.ones((token_count, token_count), dtype=jnp.bool_))
    query_wide = query_block.astype(jnp.float32)
    key_wide = key_tile.astype(jnp.float32)
    value_float = value_tile.astype(jnp.float32)
    scaled_wide = scaled_block.astype(jnp.float32)
    forward_wide = forward_narrow.astype(jnp.float32)
    back_float = back_low.astype(jnp.float32)
    raw_scores = jnp.einsum('tnd,snd->nts', query_wide, key_wide)
    scores = jnp.where(causal[None], raw_scores, 0.0).astype(jnp.bfloat16)
    scores = lax.optimization_barrier(scores).astype(jnp.float32)
    raw_grads = jnp.einsum('tnd,snd->nts', scaled_wide, value_float)
    score_gradient = jnp.where(causal[None], raw_grads, 0.0).astype(jnp.bfloat16)
    score_gradient = lax.optimization_barrier(score_gradient).astype(jnp.float32)
    local_out = jnp.einsum('epa,aev->pev', scores, value_float)
    carried_result = jnp.einsum('rwb,wbo->rwo', query_wide, forward_wide)
    attn_out = ((local_out + carried_result) * scale_block[:, None, None]).astype(jnp.bfloat16)
    query_gradient = (jnp.einsum('epa,aev->pev', score_gradient, key_wide) + jnp.einsum('hsx,smx->hsm', scaled_wide, forward_wide)).astype(jnp.bfloat16)
    grad_key = (jnp.einsum('nts,tnd->snd', score_gradient, query_wide) + jnp.einsum('snv,nvk->snk', value_float, back_float)).astype(jnp.bfloat16)
    grad_value = (jnp.einsum('nts,tnd->snd', scores, scaled_wide) + jnp.einsum('snk,nvk->snv', key_wide, back_float)).astype(jnp.bfloat16)
    return (attn_out, query_gradient, grad_key, grad_value)

def reference(queries, keys, values, out_grad):
    block_count = SEQ // BLK
    block_shape = (block_count, BLK, HEADS, DH)
    position = jnp.arange(SEQ, dtype=jnp.int32)
    position_scale = 1.0 / jnp.sqrt(jnp.float32(DH) * (position + 1).astype(jnp.float32))
    scaled = (out_grad.astype(jnp.float32) * position_scale[:, None]).astype(jnp.bfloat16)
    scaled = lax.optimization_barrier(scaled)
    query_blocks = queries.reshape(block_shape)
    key_blocks = keys.reshape(block_shape)
    value_blocks = values.reshape(block_shape)
    scaled_blocks = scaled.reshape(block_shape)
    scale_blocks = position_scale.reshape(block_count, BLK)
    forward_every, back_each = lax.map(block_states, (key_blocks, value_blocks, query_blocks, scaled_blocks))
    fwd_state = jnp.cumsum(forward_every, axis=0) - forward_every
    back_state = lax.optimization_barrier(jnp.sum(back_each, axis=0))[None] - jnp.cumsum(back_each, axis=0)
    forward_narrow = lax.optimization_barrier(fwd_state.astype(jnp.bfloat16))
    back_low = lax.optimization_barrier(back_state.astype(jnp.bfloat16))
    outputs = lax.map(block_terms, (query_blocks, key_blocks, value_blocks, scaled_blocks, forward_narrow, back_low, scale_blocks))
    attn_out = outputs[0].reshape(SEQ, HEADS * DH)
    query_gradient = outputs[1].reshape(SEQ, HEADS * DH)
    grad_key = outputs[2].reshape(SEQ, HEADS * DH)
    grad_value = outputs[3].reshape(SEQ, HEADS * DH)
    return (attn_out, query_gradient, grad_key, grad_value)
```

```python
import jax
import jax.numpy as jnp
from jax import lax
from jax.experimental import pallas as pl
from jax.experimental.pallas import tpu as pltpu
from jax.sharding import PartitionSpec as P

HEADS = 16
DH = 128
ROWS = 128
F32 = jnp.float32
BF16 = jnp.bfloat16
MESH = pl.DeviceIdType.MESH


def position_scale(span, z):
    first = (span * 16 + z) * ROWS
    position = first + lax.broadcasted_iota(jnp.int32, (ROWS, 1), 0)
    return 1.0 / jnp.sqrt(jnp.float32(DH) * (position + 1).astype(F32))


def dot(a, b, dims):
    return lax.dot_general(a, b, (dims, ((), ())), preferred_element_type=F32)


def state_kernel(
    q_ref, k_ref, v_ref, g_ref, fin,
    scaled, abuf, rbuf, cbuf, xy, cs, fout, tot, tot_in,
    a_ss, a_rs, c_ss, c_rs, f_ss, f_rs, t_ss, t_rs,
):
    span, z = lax.axis_index("span"), lax.axis_index("head")
    chip, core = span // 2, span % 2
    x, y = chip // 4, chip % 4
    pair, member = z // 2, z % 2
    half = span // 16

    barrier = pltpu.get_barrier_semaphore()

    def signal(s, zz):
        pl.semaphore_signal(barrier, inc=1, device_id={"span": s, "head": zz}, device_id_type=MESH)

    def greet(i, carry):
        signal(lax.rem(span + i, 32), z)
        signal(lax.rem(span + i, 32), pair * 2 + 1 - member)
        return carry

    lax.fori_loop(1, 32, greet, 0)
    signal(span, pair * 2 + 1 - member)

    signal(span, lax.rem(z + 2, 16))
    signal(span, lax.rem(z + 14, 16))

    scaled[...] = (g_ref[...].astype(F32) * position_scale(span, z)).astype(BF16)
    pl.semaphore_wait(barrier, 65)

    my_slot = span % 16
    home = pair * 2 + half

    def send_state(owner):
        copy = pltpu.make_async_remote_copy(
            abuf.at[owner], rbuf.at[my_slot, member], a_ss.at[owner], a_rs.at[my_slot, member],
            device_id={"span": owner, "head": home}, device_id_type=MESH,
        )
        mine = jnp.logical_and(owner == span, home == z)

        @pl.when(mine)
        def _():
            rbuf[my_slot, member] = abuf[owner]

        @pl.when(jnp.logical_not(mine))
        def _():
            copy.start()

    def states(t, carry):
        head = lax.rem(x + t % 4, 4) * 4 + lax.rem(y + t // 4, 4)
        cols = pl.ds(pl.multiple_of(head * DH, DH), DH)
        abuf[head * 2] = dot(k_ref[:, cols], v_ref[:, cols], ((0,), (0,))).astype(BF16)
        send_state(head * 2)
        abuf[head * 2 + 1] = dot(scaled[:, cols], q_ref[:, cols], ((0,), (0,))).astype(BF16)
        send_state(head * 2 + 1)
        return carry

    lax.fori_loop(0, 16, states, 0)

    def slot_of(n):
        m, cc = n // 2, n % 2
        return ((m % 2) * 4 + lax.rem(y + 4 - m // 2, 4)) * 2 + cc

    def prepare(n):
        slot = slot_of(n)
        for par in range(2):
            mine = jnp.logical_and(slot + member * 16 == span, member == par)

            @pl.when(jnp.logical_not(mine))
            def _():
                pltpu.make_async_remote_copy(
                    abuf.at[0], rbuf.at[slot, par], a_ss.at[0], a_rs.at[slot, par],
                    device_id={"span": span, "head": pair * 2 + 1 - member}, device_id_type=MESH,
                ).wait_recv()
        cbuf[slot] = rbuf[slot, 0].astype(F32) + rbuf[slot, 1].astype(F32)

    def chain_copy(way, slot):
        return pltpu.make_async_remote_copy(
            cs.at[way, slot], xy.at[way, slot], c_ss.at[way, slot], c_rs.at[way, slot],
            device_id={"span": span, "head": (jnp.minimum(z + 2, 15) if way == 0 else jnp.maximum(z - 2, 0))},
            device_id_type=MESH,
        )

    def link(way, n):
        slot = slot_of(n)
        copy = chain_copy(way, slot)
        opens = pair == (0 if way == 0 else 7)
        ends = pair == (7 if way == 0 else 0)

        @pl.when(opens)
        def _():
            xy[way, slot] = jnp.zeros((DH, DH), BF16)
            cs[way, slot] = cbuf[slot].astype(BF16)

        @pl.when(jnp.logical_not(opens))
        def _():
            copy.wait_recv()

            @pl.when(jnp.logical_not(ends))
            def _():
                cs[way, slot] = (xy[way, slot].astype(F32) + cbuf[slot]).astype(BF16)

        @pl.when(jnp.logical_not(ends))
        def _():
            copy.start()

    up_lag = jnp.maximum(0, (2 * pair - 7) * 7 // 4)
    down_lag = jnp.maximum(0, (7 - 2 * pair) * 7 // 4)

    def step(t, carry):
        @pl.when(t < 16)
        def _():
            prepare(t)

        for way, lag in ((0, up_lag), (1, down_lag)):
            n = t - lag

            @pl.when(jnp.logical_and(n >= 0, n < 16))
            def _():
                link(way, jnp.clip(n, 0, 15))

        return carry

    lax.fori_loop(0, 16 + 12, step, 0)

    def add_total(i, acc):
        return acc + xy[0, i].astype(F32) + cbuf[i] + xy[1, i].astype(F32)

    gives = member == core
    tot_copy = pltpu.make_async_remote_copy(
        tot, tot_in, t_ss, t_rs, device_id={"span": span, "head": pair * 2 + 1 - member}, device_id_type=MESH,
    )

    @pl.when(gives)
    def _():
        tot[...] = lax.fori_loop(0, 16, add_total, jnp.zeros((DH, DH), F32))
        tot_copy.start()
        tot_in[...] = jnp.zeros((DH, DH), F32)

    @pl.when(jnp.logical_not(gives))
    def _():
        tot_copy.wait_recv()

    def prefix(i, before):
        idx = core * 15 + (1 - 2 * core) * i
        near = before + xy[core, idx].astype(F32)
        fout[idx, core] = near.astype(BF16)
        fout[idx, 1 - core] = (near + rbuf[idx, core].astype(F32)).astype(BF16)
        return before + xy[0, idx].astype(F32) + cbuf[idx] + xy[1, idx].astype(F32)

    lax.fori_loop(0, 16, prefix, tot_in[...])

    def back_copy(slot, par):
        return pltpu.make_async_remote_copy(
            fout.at[slot, par], fin.at[span], f_ss.at[slot, par], f_rs.at[span],
            device_id={"span": member * 16 + slot, "head": pair * 2 + par}, device_id_type=MESH,
        )

    def returns(t, carry):
        m, cc = t // 2, t % 2
        slot = (lax.rem(m + x, 2) * 4 + lax.rem(y + m // 2, 4)) * 2 + cc
        for par in range(2):
            mine = jnp.logical_and(slot + member * 16 == span, member == par)

            @pl.when(mine)
            def _():
                fin[span] = fout[slot, par]

            @pl.when(jnp.logical_not(mine))
            def _():
                back_copy(slot, par).start()

        return carry

    lax.fori_loop(0, 16, returns, 0)

    def arrive(o, carry):
        mine = jnp.logical_and(o == span, home == z)

        @pl.when(jnp.logical_not(mine))
        def _():
            pltpu.make_async_remote_copy(
                fout.at[0, 0], fin.at[o], f_ss.at[0, 0], f_rs.at[o],
                device_id={"span": span, "head": pair * 2 + 1 - member}, device_id_type=MESH,
            ).wait_recv()

            pltpu.make_async_remote_copy(
                abuf.at[o], rbuf.at[0, 0], a_ss.at[o], a_rs.at[0, 0],
                device_id={"span": span, "head": pair * 2 + 1 - member}, device_id_type=MESH,
            ).wait_send()

        return carry

    lax.fori_loop(0, 32, arrive, 0)

    def drain(i, carry):
        for par in range(2):
            mine = jnp.logical_and(i + member * 16 == span, member == par)

            @pl.when(jnp.logical_not(mine))
            def _():
                back_copy(i, par).wait_send()

        for way, ends in ((0, pair == 7), (1, pair == 0)):

            @pl.when(jnp.logical_not(ends))
            def _():
                chain_copy(way, i).wait_send()

        return carry

    lax.fori_loop(0, 16, drain, 0)

    @pl.when(gives)
    def _():
        tot_copy.wait_send()


def states_over_devices(q, k, v, g):
    dma = pltpu.SemaphoreType.DMA
    vmem = pl.BlockSpec(memory_space=pltpu.VMEM)
    return pl.pallas_call(
        state_kernel,
        out_shape=jax.ShapeDtypeStruct((32, DH, DH), BF16),
        in_specs=[vmem] * 4,
        out_specs=vmem,
        name="carried_states",
        scratch_shapes=[
            pltpu.VMEM((ROWS, HEADS * DH), BF16),
            pltpu.VMEM((32, DH, DH), BF16),
            pltpu.VMEM((16, 2, DH, DH), BF16),
            pltpu.VMEM((16, DH, DH), F32),
            pltpu.VMEM((2, 16, DH, DH), BF16),
            pltpu.VMEM((2, 16, DH, DH), BF16),
            pltpu.VMEM((16, 2, DH, DH), BF16),
            pltpu.VMEM((DH, DH), F32),
            pltpu.VMEM((DH, DH), F32),
            dma((32,)), dma((16, 2)),
            dma((2, 16)), dma((2, 16)),
            dma((16, 2)), dma((32,)),
            dma, dma,
        ],
        compiler_params=pltpu.CompilerParams(
            collective_id=0, has_side_effects=True, vmem_limit_bytes=32 << 20
        ),
    )(q, k, v, g)


STEP_HEADS = 4


def local_kernel(q_ref, k_ref, v_ref, g_ref, f_ref, out_ref, qg_ref, gk_ref, gv_ref):
    span, z = lax.axis_index("span"), lax.axis_index("head")
    scale = position_scale(span, z)
    row = lax.broadcasted_iota(jnp.int32, (ROWS, ROWS), 0)
    col = lax.broadcasted_iota(jnp.int32, (ROWS, ROWS), 1)
    causal = col <= row
    for i in range(STEP_HEADS):
        cols = slice(i * DH, (i + 1) * DH)
        q, k, v = q_ref[:, cols], k_ref[:, cols], v_ref[:, cols]
        s = (g_ref[:, cols].astype(F32) * scale).astype(BF16)
        fwd, back = f_ref[2 * i], f_ref[2 * i + 1]
        scores = jnp.where(causal, dot(q, k, ((1,), (1,))), 0.0).astype(BF16)
        dscores = jnp.where(causal, dot(s, v, ((1,), (1,))), 0.0).astype(BF16)
        out_ref[:, cols] = ((dot(scores, v, ((1,), (0,))) + dot(q, fwd, ((1,), (0,)))) * scale).astype(BF16)
        qg_ref[:, cols] = (dot(dscores, k, ((1,), (0,))) + dot(s, fwd, ((1,), (1,)))).astype(BF16)
        gk_ref[:, cols] = (dot(dscores, q, ((0,), (0,))) + dot(v, back, ((1,), (0,)))).astype(BF16)
        gv_ref[:, cols] = (dot(scores, s, ((0,), (0,))) + dot(k, back, ((1,), (1,)))).astype(BF16)


def local_terms(q, k, v, g, states):
    wide = pl.BlockSpec((ROWS, STEP_HEADS * DH), lambda i: (0, i))
    return pl.pallas_call(
        local_kernel,
        out_shape=[jax.ShapeDtypeStruct(q.shape, BF16)] * 4,
        grid=(HEADS // STEP_HEADS,),
        in_specs=[wide] * 4 + [pl.BlockSpec((2 * STEP_HEADS, DH, DH), lambda i: (i, 0, 0))],
        out_specs=[wide] * 4,
        name="chunk_terms",
        compiler_params=pltpu.CompilerParams(vmem_limit_bytes=32 << 20),
    )(q, k, v, g, states)


def shards(queries, keys, values, out_grad):
    states = states_over_devices(queries, keys, values, out_grad)
    return tuple(local_terms(queries, keys, values, out_grad, states))


def solution(mesh):
    placed = P(("span", "head"), None)
    return jax.shard_map(
        shards, mesh=mesh, in_specs=(placed,) * 4, out_specs=(placed,) * 4, check_vma=False
    )
```

```python
import jax
import jax.numpy as jnp
from jax import lax
from jax.experimental import pallas as pl
from jax.experimental.pallas import tpu as pltpu
from jax.sharding import PartitionSpec as P

HEADS = 16
DH = 128
ROWS = 128
F32 = jnp.float32
BF16 = jnp.bfloat16
MESH = pl.DeviceIdType.MESH


def position_scale(span, z):
    first = (span * 16 + z) * ROWS
    position = first + lax.broadcasted_iota(jnp.int32, (ROWS, 1), 0)
    return 1.0 / jnp.sqrt(jnp.float32(DH) * (position + 1).astype(F32))


def dot(a, b, dims):
    return lax.dot_general(a, b, (dims, ((), ())), preferred_element_type=F32)


SLICES = 2
PART = DH // SLICES
COUNT = 8 * SLICES
LAG = 8


def state_kernel(
    q_hbm, k_hbm, v_hbm, g_hbm, fin,
    q_ref, k_ref, v_ref, g_ref, abuf, rbuf, cbuf, xy, cs, fout, tot, tot_low, row_in, sum_low, sum_in,
    l_sem, a_ss, a_rs, c_ss, c_rs, f_ss, f_rs, t_ss, t_rs,
):
    span, z = lax.axis_index("span"), lax.axis_index("head")
    chip, core = span // 2, span % 2
    x, y = chip // 4, chip % 4
    pair, member = z // 2, z % 2
    gx, gy, lx, ly = x // 2, y // 2, x % 2, y % 2
    slot_me = (lx * 2 + ly) * 2 + core
    head_me = slot_me * 2 + member

    def place(slot):
        return ((gx * 2 + slot // 4) * 4 + gy * 2 + slot // 2 % 2) * 2 + slot % 2

    def turned(n):
        return (lx + n // 4) % 2 * 4 + (ly + n // 2) % 2 * 2 + (core + n) % 2

    loads = [
        pltpu.make_async_copy(src, dst, l_sem.at[i])
        for i, (src, dst) in enumerate(((k_hbm, k_ref), (v_hbm, v_ref), (g_hbm, g_ref), (q_hbm, q_ref)))
    ]
    for load in loads:
        load.start()

    barrier = pltpu.get_barrier_semaphore()

    def signal(s, zz):
        pl.semaphore_signal(barrier, inc=1, device_id={"span": s, "head": zz}, device_id_type=MESH)

    def greet(i, carry):
        signal(place(turned(i // 2)), pair * 2 + (member + i) % 2)
        return carry

    lax.fori_loop(1, 16, greet, 0)

    def group_span(px, py):
        return ((px * 2 + lx) * 4 + py * 2 + ly) * 2 + core

    partners = [group_span(gx, 1 - gy), group_span(1 - gx, gy), group_span(1 - gx, 1 - gy)]
    for s in partners:
        signal(s, z)
    signal(span, lax.rem(z + 2, 16))
    signal(span, lax.rem(z + 14, 16))

    scale = position_scale(span, z)
    for load in loads:
        load.wait()

    def head_of(t):
        return turned(t // 2) * 2 + (member + t) % 2

    def states(t, carry):
        head = head_of(t)
        cols = pl.ds(pl.multiple_of(head * DH, DH), DH)
        scaled = (g_ref[:, cols].astype(F32) * scale).astype(BF16)
        abuf[head, 0] = dot(k_ref[:, cols], v_ref[:, cols], ((0,), (0,))).astype(BF16)
        abuf[head, 1] = dot(scaled, q_ref[:, cols], ((0,), (0,))).astype(BF16)
        return carry

    lax.fori_loop(0, 16, states, 0, unroll=2)

    pl.semaphore_wait(barrier, 20)

    def rows(part):
        return pl.ds(pl.multiple_of(part * PART, PART), PART)

    def send_states(t, carry):
        head, part = head_of(t % 16), t // 16
        src, dst = abuf.at[head, :, rows(part)], rbuf.at[slot_me, member, :, rows(part)]
        mine = head == head_me

        @pl.when(mine)
        def _():
            pltpu.make_async_copy(src, dst, a_rs.at[slot_me, part]).start()

        @pl.when(jnp.logical_not(mine))
        def _():
            pltpu.make_async_remote_copy(
                src, dst, a_ss, a_rs.at[slot_me, part],
                device_id={"span": place(head // 2), "head": pair * 2 + head % 2}, device_id_type=MESH,
            ).start()

        return carry

    lax.fori_loop(0, 16 * SLICES, send_states, 0)

    def prepare(t):
        slot, part = turned(t % 8), t // 8
        both = rbuf.at[slot, :, :, rows(part)]
        pltpu.make_async_copy(both, both, a_rs.at[slot, part]).wait()
        cbuf[slot, :, rows(part)] = (
            rbuf[slot, 0, :, rows(part)].astype(F32) + rbuf[slot, 1, :, rows(part)].astype(F32)
        )

    def link(way, n):
        slot, part = turned(n % 8), n // 8
        at = (way, slot, slice(None), rows(part))
        copy = pltpu.make_async_remote_copy(
            cs.at[at], xy.at[at], c_ss.at[way], c_rs.at[way, slot, part],
            device_id={"span": span, "head": (jnp.minimum(z + 2, 15) if way == 0 else jnp.maximum(z - 2, 0))},
            device_id_type=MESH,
        )
        opens = pair == (0 if way == 0 else 7)
        ends = pair == (7 if way == 0 else 0)

        @pl.when(opens)
        def _():
            xy[at] = jnp.zeros((2, PART, DH), BF16)
            cs[at] = cbuf[slot, :, rows(part)].astype(BF16)
            copy.start()

        @pl.when(jnp.logical_not(opens))
        def _():
            copy.wait_recv()

            @pl.when(jnp.logical_not(ends))
            def _():
                cs[at] = (xy[at].astype(F32) + cbuf[slot, :, rows(part)]).astype(BF16)
                copy.start()

    up_lag = jnp.clip((2 * pair - 7) * LAG // 2, 0, COUNT)
    down_lag = jnp.clip((7 - 2 * pair) * LAG // 2, 0, COUNT)
    last_lag = jnp.maximum(up_lag, down_lag)

    def whole(slot, r):
        return xy[0, slot, :, r].astype(F32) + cbuf[slot, :, r] + xy[1, slot, :, r].astype(F32)

    def row_copy(part):
        return pltpu.make_async_remote_copy(
            tot_low.at[:, :, rows(part)], row_in.at[:, :, rows(part)], t_ss, t_rs.at[part],
            device_id={"span": partners[0], "head": z}, device_id_type=MESH,
        )

    def sum_copy(i, part):
        return pltpu.make_async_remote_copy(
            sum_low.at[rows(part)], sum_in.at[i - 1, rows(part)], t_ss, t_rs.at[part],
            device_id={"span": partners[i], "head": z}, device_id_type=MESH,
        )

    def offer(part):
        r = rows(part)
        tot_low[:, :, r] = tot[:, :, r].astype(BF16)
        sum_low[r] = jnp.where(gx == 0, tot[0, 0, r] + tot[0, 1, r], tot[1, 0, r] + tot[1, 1, r]).astype(BF16)
        row_copy(part).start()
        sum_copy(1, part).start()
        sum_copy(2, part).start()

    def finish(part):
        r = rows(part)
        six = cs.at[0, 0:3, :, r]
        pltpu.make_async_copy(six, six, t_rs.at[part]).wait()
        far = sum_in[0, r].astype(F32) + sum_in[1, r].astype(F32)
        later, first = gy == 1, gy == 0
        low = jnp.where(gx == 1, far, 0.0) + jnp.where(later, row_in[0, 0, r].astype(F32), 0.0)
        high = jnp.where(gx == 0, far, 0.0) + jnp.where(first, row_in[1, 1, r].astype(F32), 0.0)
        low_turn = jnp.where(later, row_in[0, 1, r], row_in[0, 0, r]).astype(F32)
        high_turn = jnp.where(first, row_in[1, 0, r], row_in[1, 1, r]).astype(F32)

        def prefix(i, before):
            low, high = before
            j = 7 - i
            near = low + xy[0, i, 0, r].astype(F32)
            fout[i, 0, 0, r] = near.astype(BF16)
            fout[i, 1, 0, r] = (near + rbuf[i, 0, 0, r].astype(F32)).astype(BF16)
            low = low + xy[0, i, 0, r].astype(F32) + cbuf[i, 0, r] + xy[1, i, 0, r].astype(F32)
            near = high + xy[1, j, 1, r].astype(F32)
            fout[j, 1, 1, r] = near.astype(BF16)
            fout[j, 0, 1, r] = (near + rbuf[j, 1, 1, r].astype(F32)).astype(BF16)
            high = high + xy[0, j, 1, r].astype(F32) + cbuf[j, 1, r] + xy[1, j, 1, r].astype(F32)
            return low, high

        low, high = lax.fori_loop(0, 4, prefix, (low, high), unroll=2)
        lax.fori_loop(4, 8, prefix, (low + low_turn, high + high_turn), unroll=2)

        def returns(t, carry):
            slot, par = turned(t // 2), (member + t) % 2
            src, dst = fout.at[slot, par, :, r], fin.at[head_me, :, r]
            mine = t == 0

            @pl.when(mine)
            def _():
                pltpu.make_async_copy(src, dst, f_rs).start()

            @pl.when(jnp.logical_not(mine))
            def _():
                pltpu.make_async_remote_copy(
                    src, dst, f_ss, f_rs,
                    device_id={"span": place(slot), "head": pair * 2 + par}, device_id_type=MESH,
                ).start()

            return carry

        lax.fori_loop(0, 16, returns, 0)

    def step(t, carry):
        @pl.when(t < COUNT)
        def _():
            prepare(t)

        for way, lag in ((0, up_lag), (1, down_lag)):
            n = t - lag

            @pl.when(jnp.logical_and(n >= 0, n < COUNT))
            def _():
                link(way, jnp.clip(n, 0, COUNT - 1))

        done = t - last_lag

        @pl.when(jnp.logical_and(done >= 0, done < COUNT))
        def _():
            at = jnp.clip(done, 0, COUNT - 1)
            part = at // 8
            r = rows(part)
            slot = turned(at % 8)
            tot[:, slot // 4, r] = tot[:, slot // 4, r] + whole(slot, r)

            @pl.when(at % 8 == 7)
            def _():
                offer(part)

        ready = done - 1

        @pl.when(jnp.logical_and(ready >= 7, jnp.logical_and(ready < COUNT, ready % 8 == 7)))
        def _():
            finish(jnp.clip(ready, 0, COUNT - 1) // 8)

        return carry

    tot[...] = jnp.zeros((2, 2, DH, DH), F32)
    lax.fori_loop(0, 2 * COUNT + 1, step, 0)

    pltpu.make_async_copy(fin, fin, f_rs).wait()

    most = abuf.at[pl.ds(0, 15)]
    pltpu.make_async_copy(most, most, a_ss).wait()
    pltpu.make_async_copy(most, most, f_ss).wait()

    for way, ends in ((0, pair == 7), (1, pair == 0)):

        @pl.when(jnp.logical_not(ends))
        def _():
            pltpu.make_async_copy(cs.at[way], cs.at[way], c_ss.at[way]).wait()

    pltpu.make_async_copy(cs.at[0, 0:3], cs.at[0, 0:3], t_ss).wait()


def states_over_devices(q, k, v, g):
    dma = pltpu.SemaphoreType.DMA
    return pl.pallas_call(
        state_kernel,
        out_shape=jax.ShapeDtypeStruct((16, 2, DH, DH), BF16),
        in_specs=[pl.BlockSpec(memory_space=pltpu.HBM)] * 4,
        out_specs=pl.BlockSpec(memory_space=pltpu.VMEM),
        name="carried_states",
        scratch_shapes=[pltpu.VMEM((ROWS, HEADS * DH), BF16)] * 4
        + [
            pltpu.VMEM((16, 2, DH, DH), BF16),
            pltpu.VMEM((8, 2, 2, DH, DH), BF16),
            pltpu.VMEM((8, 2, DH, DH), F32),
            pltpu.VMEM((2, 8, 2, DH, DH), BF16),
            pltpu.VMEM((2, 8, 2, DH, DH), BF16),
            pltpu.VMEM((8, 2, 2, DH, DH), BF16),
            pltpu.VMEM((2, 2, DH, DH), F32),
            pltpu.VMEM((2, 2, DH, DH), BF16),
            pltpu.VMEM((2, 2, DH, DH), BF16),
            pltpu.VMEM((DH, DH), BF16),
            pltpu.VMEM((2, DH, DH), BF16),
            dma((4,)),
            dma, dma((8, SLICES)),
            dma((2,)), dma((2, 8, SLICES)),
            dma, dma,
            dma, dma((SLICES,)),
        ],
        compiler_params=pltpu.CompilerParams(
            collective_id=0, has_side_effects=True, vmem_limit_bytes=56 << 20
        ),
    )(q, k, v, g)


STEP_HEADS = 4


def local_kernel(q_ref, k_ref, v_ref, g_ref, f_ref, out_ref, qg_ref, gk_ref, gv_ref):
    span, z = lax.axis_index("span"), lax.axis_index("head")
    scale = position_scale(span, z)
    row = lax.broadcasted_iota(jnp.int32, (ROWS, ROWS), 0)
    col = lax.broadcasted_iota(jnp.int32, (ROWS, ROWS), 1)
    causal = col <= row
    for i in range(STEP_HEADS):
        cols = slice(i * DH, (i + 1) * DH)
        q, k, v = q_ref[:, cols], k_ref[:, cols], v_ref[:, cols]
        s = (g_ref[:, cols].astype(F32) * scale).astype(BF16)
        head = pl.program_id(0) * STEP_HEADS + i
        fwd, back = f_ref[head, 0], f_ref[head, 1]
        scores = jnp.where(causal, dot(q, k, ((1,), (1,))), 0.0).astype(BF16)
        dscores = jnp.where(causal, dot(s, v, ((1,), (1,))), 0.0).astype(BF16)
        out_ref[:, cols] = ((dot(scores, v, ((1,), (0,))) + dot(q, fwd, ((1,), (0,)))) * scale).astype(BF16)
        qg_ref[:, cols] = (dot(dscores, k, ((1,), (0,))) + dot(s, fwd, ((1,), (1,)))).astype(BF16)
        gk_ref[:, cols] = (dot(dscores, q, ((0,), (0,))) + dot(v, back, ((1,), (0,)))).astype(BF16)
        gv_ref[:, cols] = (dot(scores, s, ((0,), (0,))) + dot(k, back, ((1,), (1,)))).astype(BF16)


def local_terms(q, k, v, g, states):
    wide = pl.BlockSpec((ROWS, STEP_HEADS * DH), lambda i: (0, i))
    return pl.pallas_call(
        local_kernel,
        out_shape=[jax.ShapeDtypeStruct(q.shape, BF16)] * 4,
        grid=(HEADS // STEP_HEADS,),
        in_specs=[wide] * 4 + [pl.BlockSpec(memory_space=pltpu.VMEM)],
        out_specs=[wide] * 4,
        name="chunk_terms",
        compiler_params=pltpu.CompilerParams(vmem_limit_bytes=32 << 20),
    )(q, k, v, g, states)


def shards(queries, keys, values, out_grad):
    states = states_over_devices(queries, keys, values, out_grad)
    return tuple(local_terms(queries, keys, values, out_grad, states))


def solution(mesh):
    placed = P(("span", "head"), None)
    return jax.shard_map(
        shards, mesh=mesh, in_specs=(placed,) * 4, out_specs=(placed,) * 4, check_vma=False
    )
```

```python
import jax
import jax.numpy as jnp
from jax import lax
from jax.experimental import pallas as pl
from jax.experimental.pallas import tpu as pltpu
from jax.sharding import PartitionSpec as P

HEADS = 16
DH = 128
ROWS = 128
F32 = jnp.float32
BF16 = jnp.bfloat16
MESH = pl.DeviceIdType.MESH


def position_scale(span, z):
    first = (span * 16 + z) * ROWS
    position = first + lax.broadcasted_iota(jnp.int32, (ROWS, 1), 0)
    return 1.0 / jnp.sqrt(jnp.float32(DH) * (position + 1).astype(F32))


def dot(a, b, dims):
    return lax.dot_general(a, b, (dims, ((), ())), preferred_element_type=F32)


SLICES = 2
PART = DH // SLICES
COUNT = 8 * SLICES
LAG = 8


def state_kernel(
    q_hbm, k_hbm, v_hbm, g_hbm, fin,
    q_ref, k_ref, v_ref, g_ref, abuf, rbuf, xy, cs, fout, tot, tot_low, row_in, sum_low, sum_in,
    l_sem, a_ss, a_rs, c_ss, c_rs, f_ss, f_rs, t_ss, t_rs,
):
    span, z = lax.axis_index("span"), lax.axis_index("head")
    chip, core = span >> 1, span & 1
    x, y = chip >> 2, chip & 3
    pair, member = z >> 1, z & 1
    gx, gy, lx, ly = x >> 1, y >> 1, x & 1, y & 1
    slot_me = (lx * 2 + ly) * 2 + core
    head_me = slot_me * 2 + member

    corner = gx * 16 + gy * 4

    def place(slot):
        return corner + (slot >> 2) * 8 + (slot & 3)

    def turned(n):
        return slot_me ^ n

    loads = [
        pltpu.make_async_copy(src, dst, l_sem.at[i])
        for i, (src, dst) in enumerate(((k_hbm, k_ref), (v_hbm, v_ref), (g_hbm, g_ref), (q_hbm, q_ref)))
    ]
    for load in loads:
        load.start()

    barrier = pltpu.get_barrier_semaphore()

    def signal(s, zz):
        pl.semaphore_signal(barrier, inc=1, device_id={"span": s, "head": zz}, device_id_type=MESH)

    def greet(i, carry):
        signal(place(turned(i >> 1)), pair * 2 + (member ^ (i & 1)))
        return carry

    lax.fori_loop(1, 16, greet, 0)

    def group_span(px, py):
        return ((px * 2 + lx) * 4 + py * 2 + ly) * 2 + core

    partners = [group_span(gx, 1 - gy), group_span(1 - gx, gy), group_span(1 - gx, 1 - gy)]
    for s in partners:
        signal(s, z)
    signal(span, lax.rem(z + 2, 16))
    signal(span, lax.rem(z + 14, 16))

    scale = position_scale(span, z)
    for load in loads:
        load.wait()

    def head_of(t):
        return head_me ^ t

    def states(t, carry):
        head = head_of(t)
        cols = pl.ds(pl.multiple_of(head * DH, DH), DH)
        scaled = (g_ref[:, cols].astype(F32) * scale).astype(BF16)
        abuf[head, 0] = dot(k_ref[:, cols], v_ref[:, cols], ((0,), (0,))).astype(BF16)
        abuf[head, 1] = dot(scaled, q_ref[:, cols], ((0,), (0,))).astype(BF16)
        return carry

    lax.fori_loop(0, 16, states, 0, unroll=2)

    pl.semaphore_wait(barrier, 20)

    def rows(part):
        return pl.ds(pl.multiple_of(part * PART, PART), PART)

    def send_states(t, carry):
        head, part = head_of(t & 15), t >> 4
        src, dst = abuf.at[head, :, rows(part)], rbuf.at[slot_me, member, :, rows(part)]
        mine = head == head_me

        @pl.when(mine)
        def _():
            pltpu.make_async_copy(src, dst, a_rs.at[slot_me, part]).start()

        @pl.when(jnp.logical_not(mine))
        def _():
            pltpu.make_async_remote_copy(
                src, dst, a_ss, a_rs.at[slot_me, part],
                device_id={"span": place(head >> 1), "head": pair * 2 + (head & 1)}, device_id_type=MESH,
            ).start()

        return carry

    lax.fori_loop(0, 16 * SLICES, send_states, 0)

    def prepare(t):
        slot, part = turned(t & 7), t >> 3
        both = rbuf.at[slot, :, :, rows(part)]
        pltpu.make_async_copy(both, both, a_rs.at[slot, part]).wait()

    def both_chunks(slot, r):
        return rbuf[slot, 0, :, r].astype(F32) + rbuf[slot, 1, :, r].astype(F32)

    def link(way, n):
        slot, part = turned(n & 7), n >> 3
        at = (way, slot, slice(None), rows(part))
        copy = pltpu.make_async_remote_copy(
            cs.at[at], xy.at[at], c_ss.at[way], c_rs.at[way, slot, part],
            device_id={"span": span, "head": (jnp.minimum(z + 2, 15) if way == 0 else jnp.maximum(z - 2, 0))},
            device_id_type=MESH,
        )
        opens = pair == (0 if way == 0 else 7)
        ends = pair == (7 if way == 0 else 0)

        @pl.when(opens)
        def _():
            xy[at] = jnp.zeros((2, PART, DH), BF16)
            cs[at] = both_chunks(slot, rows(part)).astype(BF16)
            copy.start()

        @pl.when(jnp.logical_not(opens))
        def _():
            copy.wait_recv()

            @pl.when(jnp.logical_not(ends))
            def _():
                cs[at] = (xy[at].astype(F32) + both_chunks(slot, rows(part))).astype(BF16)
                copy.start()

    up_lag = jnp.clip(((2 * pair - 7) * LAG) >> 1, 0, COUNT)
    down_lag = jnp.clip(((7 - 2 * pair) * LAG) >> 1, 0, COUNT)
    last_lag = jnp.maximum(up_lag, down_lag)

    def whole(slot, r):
        return xy[0, slot, :, r].astype(F32) + both_chunks(slot, r) + xy[1, slot, :, r].astype(F32)

    def row_copy(part):
        return pltpu.make_async_remote_copy(
            tot_low.at[:, :, rows(part)], row_in.at[:, :, rows(part)], t_ss, t_rs.at[part],
            device_id={"span": partners[0], "head": z}, device_id_type=MESH,
        )

    def sum_copy(i, part):
        return pltpu.make_async_remote_copy(
            sum_low.at[rows(part)], sum_in.at[i - 1, rows(part)], t_ss, t_rs.at[part],
            device_id={"span": partners[i], "head": z}, device_id_type=MESH,
        )

    def offer(part):
        r = rows(part)
        tot_low[:, :, r] = tot[:, :, r].astype(BF16)
        sum_low[r] = jnp.where(gx == 0, tot[0, 0, r] + tot[0, 1, r], tot[1, 0, r] + tot[1, 1, r]).astype(BF16)
        row_copy(part).start()
        sum_copy(1, part).start()
        sum_copy(2, part).start()

    def finish(part):
        r = rows(part)
        six = cs.at[0, 0:3, :, r]
        pltpu.make_async_copy(six, six, t_rs.at[part]).wait()
        far = sum_in[0, r].astype(F32) + sum_in[1, r].astype(F32)
        later, first = gy == 1, gy == 0
        low = jnp.where(gx == 1, far, 0.0) + jnp.where(later, row_in[0, 0, r].astype(F32), 0.0)
        high = jnp.where(gx == 0, far, 0.0) + jnp.where(first, row_in[1, 1, r].astype(F32), 0.0)
        low_turn = jnp.where(later, row_in[0, 1, r], row_in[0, 0, r]).astype(F32)
        high_turn = jnp.where(first, row_in[1, 0, r], row_in[1, 1, r]).astype(F32)

        def prefix(i, before):
            low, high = before
            j = 7 - i
            near = low + xy[0, i, 0, r].astype(F32)
            fout[i, 0, 0, r] = near.astype(BF16)
            near = near + rbuf[i, 0, 0, r].astype(F32)
            fout[i, 1, 0, r] = near.astype(BF16)
            low = near + rbuf[i, 1, 0, r].astype(F32) + xy[1, i, 0, r].astype(F32)
            near = high + xy[1, j, 1, r].astype(F32)
            fout[j, 1, 1, r] = near.astype(BF16)
            near = near + rbuf[j, 1, 1, r].astype(F32)
            fout[j, 0, 1, r] = near.astype(BF16)
            high = near + rbuf[j, 0, 1, r].astype(F32) + xy[0, j, 1, r].astype(F32)
            return low, high

        low, high = lax.fori_loop(0, 4, prefix, (low, high), unroll=2)
        lax.fori_loop(4, 8, prefix, (low + low_turn, high + high_turn), unroll=2)

        def returns(t, carry):
            slot, par = turned(t >> 1), member ^ (t & 1)
            src, dst = fout.at[slot, par, :, r], fin.at[head_me, :, r]
            mine = t == 0

            @pl.when(mine)
            def _():
                pltpu.make_async_copy(src, dst, f_rs).start()

            @pl.when(jnp.logical_not(mine))
            def _():
                pltpu.make_async_remote_copy(
                    src, dst, f_ss, f_rs,
                    device_id={"span": place(slot), "head": pair * 2 + par}, device_id_type=MESH,
                ).start()

            return carry

        lax.fori_loop(0, 16, returns, 0)

    def step(t, carry):
        @pl.when(t < COUNT)
        def _():
            prepare(t)

        for way, lag in ((0, up_lag), (1, down_lag)):
            n = t - lag

            @pl.when(jnp.logical_and(n >= 0, n < COUNT))
            def _():
                link(way, jnp.clip(n, 0, COUNT - 1))

        done = t - last_lag

        @pl.when(jnp.logical_and(done >= 0, done < COUNT))
        def _():
            at = jnp.clip(done, 0, COUNT - 1)
            part = at >> 3
            r = rows(part)
            slot = turned(at & 7)
            tot[:, slot >> 2, r] = tot[:, slot >> 2, r] + whole(slot, r)

            @pl.when(at & 7 == 7)
            def _():
                offer(part)

        ready = done - 1

        @pl.when(jnp.logical_and(ready >= 7, jnp.logical_and(ready < COUNT, ready & 7 == 7)))
        def _():
            finish(jnp.clip(ready, 0, COUNT - 1) >> 3)

        return carry

    tot[...] = jnp.zeros((2, 2, DH, DH), F32)
    lax.fori_loop(0, 2 * COUNT + 1, step, 0)

    pltpu.make_async_copy(fin, fin, f_rs).wait()

    most = abuf.at[pl.ds(0, 15)]
    pltpu.make_async_copy(most, most, a_ss).wait()
    pltpu.make_async_copy(most, most, f_ss).wait()

    for way, ends in ((0, pair == 7), (1, pair == 0)):

        @pl.when(jnp.logical_not(ends))
        def _():
            pltpu.make_async_copy(cs.at[way], cs.at[way], c_ss.at[way]).wait()

    pltpu.make_async_copy(cs.at[0, 0:3], cs.at[0, 0:3], t_ss).wait()


def states_over_devices(q, k, v, g):
    dma = pltpu.SemaphoreType.DMA
    return pl.pallas_call(
        state_kernel,
        out_shape=jax.ShapeDtypeStruct((16, 2, DH, DH), BF16),
        in_specs=[pl.BlockSpec(memory_space=pltpu.HBM)] * 4,
        out_specs=pl.BlockSpec(memory_space=pltpu.VMEM),
        name="carried_states",
        scratch_shapes=[pltpu.VMEM((ROWS, HEADS * DH), BF16)] * 4
        + [
            pltpu.VMEM((16, 2, DH, DH), BF16),
            pltpu.VMEM((8, 2, 2, DH, DH), BF16),
            pltpu.VMEM((2, 8, 2, DH, DH), BF16),
            pltpu.VMEM((2, 8, 2, DH, DH), BF16),
            pltpu.VMEM((8, 2, 2, DH, DH), BF16),
            pltpu.VMEM((2, 2, DH, DH), F32),
            pltpu.VMEM((2, 2, DH, DH), BF16),
            pltpu.VMEM((2, 2, DH, DH), BF16),
            pltpu.VMEM((DH, DH), BF16),
            pltpu.VMEM((2, DH, DH), BF16),
            dma((4,)),
            dma, dma((8, SLICES)),
            dma((2,)), dma((2, 8, SLICES)),
            dma, dma,
            dma, dma((SLICES,)),
        ],
        compiler_params=pltpu.CompilerParams(
            collective_id=0, has_side_effects=True, vmem_limit_bytes=56 << 20
        ),
    )(q, k, v, g)


STEP_HEADS = 4


def local_kernel(q_ref, k_ref, v_ref, g_ref, f_ref, out_ref, qg_ref, gk_ref, gv_ref):
    span, z = lax.axis_index("span"), lax.axis_index("head")
    scale = position_scale(span, z)
    row = lax.broadcasted_iota(jnp.int32, (ROWS, ROWS), 0)
    col = lax.broadcasted_iota(jnp.int32, (ROWS, ROWS), 1)
    causal = col <= row
    for i in range(STEP_HEADS):
        cols = slice(i * DH, (i + 1) * DH)
        q, k, v = q_ref[:, cols], k_ref[:, cols], v_ref[:, cols]
        s = (g_ref[:, cols].astype(F32) * scale).astype(BF16)
        head = pl.program_id(0) * STEP_HEADS + i
        fwd, back = f_ref[head, 0], f_ref[head, 1]
        scores = jnp.where(causal, dot(q, k, ((1,), (1,))), 0.0).astype(BF16)
        dscores = jnp.where(causal, dot(s, v, ((1,), (1,))), 0.0).astype(BF16)
        out_ref[:, cols] = ((dot(scores, v, ((1,), (0,))) + dot(q, fwd, ((1,), (0,)))) * scale).astype(BF16)
        qg_ref[:, cols] = (dot(dscores, k, ((1,), (0,))) + dot(s, fwd, ((1,), (1,)))).astype(BF16)
        gk_ref[:, cols] = (dot(dscores, q, ((0,), (0,))) + dot(v, back, ((1,), (0,)))).astype(BF16)
        gv_ref[:, cols] = (dot(scores, s, ((0,), (0,))) + dot(k, back, ((1,), (1,)))).astype(BF16)


def local_terms(q, k, v, g, states):
    wide = pl.BlockSpec((ROWS, STEP_HEADS * DH), lambda i: (0, i))
    return pl.pallas_call(
        local_kernel,
        out_shape=[jax.ShapeDtypeStruct(q.shape, BF16)] * 4,
        grid=(HEADS // STEP_HEADS,),
        in_specs=[wide] * 4 + [pl.BlockSpec(memory_space=pltpu.VMEM)],
        out_specs=[wide] * 4,
        name="chunk_terms",
        compiler_params=pltpu.CompilerParams(vmem_limit_bytes=32 << 20),
    )(q, k, v, g, states)


def shards(queries, keys, values, out_grad):
    states = states_over_devices(queries, keys, values, out_grad)
    return tuple(local_terms(queries, keys, values, out_grad, states))


def solution(mesh):
    placed = P(("span", "head"), None)
    return jax.shard_map(
        shards, mesh=mesh, in_specs=(placed,) * 4, out_specs=(placed,) * 4, check_vma=False
    )
```

```python
import jax
import jax.numpy as jnp
from jax import lax
from jax.experimental import pallas as pl
from jax.experimental.pallas import tpu as pltpu
from jax.sharding import PartitionSpec as P

HEADS = 16
DH = 128
ROWS = 128
F32 = jnp.float32
BF16 = jnp.bfloat16
MESH = pl.DeviceIdType.MESH


def position_scale(span, z):
    first = (span * 16 + z) * ROWS
    position = first + lax.broadcasted_iota(jnp.int32, (ROWS, 1), 0)
    return 1.0 / jnp.sqrt(jnp.float32(DH) * (position + 1).astype(F32))


def dot(a, b, dims):
    return lax.dot_general(a, b, (dims, ((), ())), preferred_element_type=F32)


SLICES = 2
PART = DH // SLICES
COUNT = 8 * SLICES
LAG = 8


def state_kernel(
    q_hbm, k_hbm, v_hbm, g_hbm, fin,
    q_ref, k_ref, v_ref, g_ref, abuf, rbuf, xy, cs, fout, tot, tot_low, row_in, sum_low, sum_in,
    l_sem, a_ss, a_rs, c_ss, c_rs, f_ss, f_rs, t_ss, t_rs,
):
    span, z = lax.axis_index("span"), lax.axis_index("head")
    chip, core = span >> 1, span & 1
    x, y = chip >> 2, chip & 3
    pair, member = z >> 1, z & 1
    gx, gy, lx, ly = x >> 1, y >> 1, x & 1, y & 1
    slot_me = (lx * 2 + ly) * 2 + core
    head_me = slot_me * 2 + member

    corner = gx * 16 + gy * 4

    def place(slot):
        return corner + (slot >> 2) * 8 + (slot & 3)

    def turned(n):
        return slot_me ^ n

    loads = [
        pltpu.make_async_copy(src, dst, l_sem.at[i])
        for i, (src, dst) in enumerate(((k_hbm, k_ref), (v_hbm, v_ref), (g_hbm, g_ref), (q_hbm, q_ref)))
    ]
    for load in loads:
        load.start()

    barrier = pltpu.get_barrier_semaphore()

    def signal(s, zz):
        pl.semaphore_signal(barrier, inc=1, device_id={"span": s, "head": zz}, device_id_type=MESH)

    def greet(i, carry):
        signal(place(turned(i >> 1)), pair * 2 + (member ^ (i & 1)))
        return carry

    lax.fori_loop(1, 16, greet, 0)

    def group_span(px, py):
        return ((px * 2 + lx) * 4 + py * 2 + ly) * 2 + core

    partners = [group_span(gx, 1 - gy), group_span(1 - gx, gy), group_span(1 - gx, 1 - gy)]
    for s in partners:
        signal(s, z)
    signal(span, lax.rem(z + 2, 16))
    signal(span, lax.rem(z + 14, 16))

    scale = position_scale(span, z)
    for load in loads:
        load.wait()

    def head_of(t):
        return head_me ^ t

    def states(t, carry):
        head = head_of(t)
        cols = pl.ds(pl.multiple_of(head * DH, DH), DH)
        scaled = (g_ref[:, cols].astype(F32) * scale).astype(BF16)
        abuf[head, 0] = dot(k_ref[:, cols], v_ref[:, cols], ((0,), (0,))).astype(BF16)
        abuf[head, 1] = dot(scaled, q_ref[:, cols], ((0,), (0,))).astype(BF16)
        return carry

    lax.fori_loop(0, 16, states, 0, unroll=2)

    pl.semaphore_wait(barrier, 20)

    def rows(part):
        return pl.ds(pl.multiple_of(part * PART, PART), PART)

    def send_states(t, carry):
        head, part = head_of(t & 15), t >> 4
        src, dst = abuf.at[head, :, rows(part)], rbuf.at[slot_me, member, :, rows(part)]
        mine = head == head_me

        @pl.when(mine)
        def _():
            pltpu.make_async_copy(src, dst, a_rs.at[slot_me, part]).start()

        @pl.when(jnp.logical_not(mine))
        def _():
            pltpu.make_async_remote_copy(
                src, dst, a_ss, a_rs.at[slot_me, part],
                device_id={"span": place(head >> 1), "head": pair * 2 + (head & 1)}, device_id_type=MESH,
            ).start()

        return carry

    lax.fori_loop(0, 16 * SLICES, send_states, 0)

    def prepare(t):
        slot, part = turned(t & 7), t >> 3
        both = rbuf.at[slot, :, :, rows(part)]
        pltpu.make_async_copy(both, both, a_rs.at[slot, part]).wait()

    def both_chunks(slot, r):
        return rbuf[slot, 0, :, r].astype(F32) + rbuf[slot, 1, :, r].astype(F32)

    def link(way, n):
        slot, part = turned(n & 7), n >> 3
        at = (way, slot, slice(None), rows(part))
        copy = pltpu.make_async_remote_copy(
            cs.at[at], xy.at[at], c_ss.at[way], c_rs.at[way, slot, part],
            device_id={"span": span, "head": (jnp.minimum(z + 2, 15) if way == 0 else jnp.maximum(z - 2, 0))},
            device_id_type=MESH,
        )
        opens = pair == (0 if way == 0 else 7)
        ends = pair == (7 if way == 0 else 0)

        @pl.when(opens)
        def _():
            xy[at] = jnp.zeros((2, PART, DH), BF16)
            cs[at] = both_chunks(slot, rows(part)).astype(BF16)
            copy.start()

        @pl.when(jnp.logical_not(opens))
        def _():
            copy.wait_recv()

            @pl.when(jnp.logical_not(ends))
            def _():
                cs[at] = (xy[at].astype(F32) + both_chunks(slot, rows(part))).astype(BF16)
                copy.start()

    up_lag = jnp.clip(((2 * pair - 7) * LAG) >> 1, 0, COUNT)
    down_lag = jnp.clip(((7 - 2 * pair) * LAG) >> 1, 0, COUNT)
    last_lag = jnp.maximum(up_lag, down_lag)

    def whole(slot, r):
        return xy[0, slot, :, r].astype(F32) + both_chunks(slot, r) + xy[1, slot, :, r].astype(F32)

    def row_copy(part):
        return pltpu.make_async_remote_copy(
            tot_low.at[:, :, rows(part)], row_in.at[:, :, rows(part)], t_ss, t_rs.at[part],
            device_id={"span": partners[0], "head": z}, device_id_type=MESH,
        )

    def sum_copy(i, part):
        return pltpu.make_async_remote_copy(
            sum_low.at[rows(part)], sum_in.at[i - 1, rows(part)], t_ss, t_rs.at[part],
            device_id={"span": partners[i], "head": z}, device_id_type=MESH,
        )

    def offer(part):
        r = rows(part)
        tot_low[:, :, r] = tot[:, :, r].astype(BF16)
        sum_low[r] = jnp.where(gx == 0, tot[0, 0, r] + tot[0, 1, r], tot[1, 0, r] + tot[1, 1, r]).astype(BF16)
        row_copy(part).start()
        sum_copy(1, part).start()
        sum_copy(2, part).start()

    def finish(part):
        r = rows(part)
        six = cs.at[0, 0:3, :, r]
        pltpu.make_async_copy(six, six, t_rs.at[part]).wait()
        far = sum_in[0, r].astype(F32) + sum_in[1, r].astype(F32)
        later, first = gy == 1, gy == 0
        low = jnp.where(gx == 1, far, 0.0) + jnp.where(later, row_in[0, 0, r].astype(F32), 0.0)
        high = jnp.where(gx == 0, far, 0.0) + jnp.where(first, row_in[1, 1, r].astype(F32), 0.0)
        low_turn = jnp.where(later, row_in[0, 1, r], row_in[0, 0, r]).astype(F32)
        high_turn = jnp.where(first, row_in[1, 0, r], row_in[1, 1, r]).astype(F32)

        def prefix(i, before):
            low, high = before
            j = 7 - i
            near = low + xy[0, i, 0, r].astype(F32)
            fout[i, 0, 0, r] = near.astype(BF16)
            near = near + rbuf[i, 0, 0, r].astype(F32)
            fout[i, 1, 0, r] = near.astype(BF16)
            low = near + rbuf[i, 1, 0, r].astype(F32) + xy[1, i, 0, r].astype(F32)
            near = high + xy[1, j, 1, r].astype(F32)
            fout[j, 1, 1, r] = near.astype(BF16)
            near = near + rbuf[j, 1, 1, r].astype(F32)
            fout[j, 0, 1, r] = near.astype(BF16)
            high = near + rbuf[j, 0, 1, r].astype(F32) + xy[0, j, 1, r].astype(F32)
            return low, high

        low, high = lax.fori_loop(0, 4, prefix, (low, high), unroll=2)
        lax.fori_loop(4, 8, prefix, (low + low_turn, high + high_turn), unroll=2)

        def returns(t, carry):
            slot, par = turned(t >> 1), member ^ (t & 1)
            src, dst = fout.at[slot, par, :, r], fin.at[head_me, :, r]
            mine = t == 0

            @pl.when(mine)
            def _():
                pltpu.make_async_copy(src, dst, f_rs).start()

            @pl.when(jnp.logical_not(mine))
            def _():
                pltpu.make_async_remote_copy(
                    src, dst, f_ss, f_rs,
                    device_id={"span": place(slot), "head": pair * 2 + par}, device_id_type=MESH,
                ).start()

            return carry

        lax.fori_loop(0, 16, returns, 0)

    def step(t, carry):
        @pl.when(t < COUNT)
        def _():
            prepare(t)

        for way, lag in ((0, up_lag), (1, down_lag)):
            n = t - lag

            @pl.when(jnp.logical_and(n >= 0, n < COUNT))
            def _():
                link(way, jnp.clip(n, 0, COUNT - 1))

        done = t - last_lag

        @pl.when(jnp.logical_and(done >= 0, done < COUNT))
        def _():
            at = jnp.clip(done, 0, COUNT - 1)
            part = at >> 3
            r = rows(part)
            slot = turned(at & 7)
            tot[:, slot >> 2, r] = tot[:, slot >> 2, r] + whole(slot, r)

            @pl.when(at & 7 == 7)
            def _():
                offer(part)

        ready = done - 9

        @pl.when(jnp.logical_and(ready >= 7, jnp.logical_and(ready < COUNT, ready & 7 == 7)))
        def _():
            finish(jnp.clip(ready, 0, COUNT - 1) >> 3)

        return carry

    tot[...] = jnp.zeros((2, 2, DH, DH), F32)
    lax.fori_loop(0, 2 * COUNT + 9, step, 0)

    pltpu.make_async_copy(fin, fin, f_rs).wait()

    most = abuf.at[pl.ds(0, 15)]
    pltpu.make_async_copy(most, most, a_ss).wait()
    pltpu.make_async_copy(most, most, f_ss).wait()

    for way, ends in ((0, pair == 7), (1, pair == 0)):

        @pl.when(jnp.logical_not(ends))
        def _():
            pltpu.make_async_copy(cs.at[way], cs.at[way], c_ss.at[way]).wait()

    pltpu.make_async_copy(cs.at[0, 0:3], cs.at[0, 0:3], t_ss).wait()


def states_over_devices(q, k, v, g):
    dma = pltpu.SemaphoreType.DMA
    return pl.pallas_call(
        state_kernel,
        out_shape=jax.ShapeDtypeStruct((16, 2, DH, DH), BF16),
        in_specs=[pl.BlockSpec(memory_space=pltpu.HBM)] * 4,
        out_specs=pl.BlockSpec(memory_space=pltpu.VMEM),
        name="carried_states",
        scratch_shapes=[pltpu.VMEM((ROWS, HEADS * DH), BF16)] * 4
        + [
            pltpu.VMEM((16, 2, DH, DH), BF16),
            pltpu.VMEM((8, 2, 2, DH, DH), BF16),
            pltpu.VMEM((2, 8, 2, DH, DH), BF16),
            pltpu.VMEM((2, 8, 2, DH, DH), BF16),
            pltpu.VMEM((8, 2, 2, DH, DH), BF16),
            pltpu.VMEM((2, 2, DH, DH), F32),
            pltpu.VMEM((2, 2, DH, DH), BF16),
            pltpu.VMEM((2, 2, DH, DH), BF16),
            pltpu.VMEM((DH, DH), BF16),
            pltpu.VMEM((2, DH, DH), BF16),
            dma((4,)),
            dma, dma((8, SLICES)),
            dma((2,)), dma((2, 8, SLICES)),
            dma, dma,
            dma, dma((SLICES,)),
        ],
        compiler_params=pltpu.CompilerParams(
            collective_id=0, has_side_effects=True, vmem_limit_bytes=56 << 20
        ),
    )(q, k, v, g)


STEP_HEADS = 4


def local_kernel(q_ref, k_ref, v_ref, g_ref, f_ref, out_ref, qg_ref, gk_ref, gv_ref):
    span, z = lax.axis_index("span"), lax.axis_index("head")
    scale = position_scale(span, z)
    row = lax.broadcasted_iota(jnp.int32, (ROWS, ROWS), 0)
    col = lax.broadcasted_iota(jnp.int32, (ROWS, ROWS), 1)
    causal = col <= row
    for i in range(STEP_HEADS):
        cols = slice(i * DH, (i + 1) * DH)
        q, k, v = q_ref[:, cols], k_ref[:, cols], v_ref[:, cols]
        s = (g_ref[:, cols].astype(F32) * scale).astype(BF16)
        head = pl.program_id(0) * STEP_HEADS + i
        fwd, back = f_ref[head, 0], f_ref[head, 1]
        scores = jnp.where(causal, dot(q, k, ((1,), (1,))), 0.0).astype(BF16)
        dscores = jnp.where(causal, dot(s, v, ((1,), (1,))), 0.0).astype(BF16)
        out_ref[:, cols] = ((dot(scores, v, ((1,), (0,))) + dot(q, fwd, ((1,), (0,)))) * scale).astype(BF16)
        qg_ref[:, cols] = (dot(dscores, k, ((1,), (0,))) + dot(s, fwd, ((1,), (1,)))).astype(BF16)
        gk_ref[:, cols] = (dot(dscores, q, ((0,), (0,))) + dot(v, back, ((1,), (0,)))).astype(BF16)
        gv_ref[:, cols] = (dot(scores, s, ((0,), (0,))) + dot(k, back, ((1,), (1,)))).astype(BF16)


def local_terms(q, k, v, g, states):
    wide = pl.BlockSpec((ROWS, STEP_HEADS * DH), lambda i: (0, i))
    return pl.pallas_call(
        local_kernel,
        out_shape=[jax.ShapeDtypeStruct(q.shape, BF16)] * 4,
        grid=(HEADS // STEP_HEADS,),
        in_specs=[wide] * 4 + [pl.BlockSpec(memory_space=pltpu.VMEM)],
        out_specs=[wide] * 4,
        name="chunk_terms",
        compiler_params=pltpu.CompilerParams(vmem_limit_bytes=32 << 20),
    )(q, k, v, g, states)


def shards(queries, keys, values, out_grad):
    states = states_over_devices(queries, keys, values, out_grad)
    return tuple(local_terms(queries, keys, values, out_grad, states))


def solution(mesh):
    placed = P(("span", "head"), None)
    return jax.shard_map(
        shards, mesh=mesh, in_specs=(placed,) * 4, out_specs=(placed,) * 4, check_vma=False
    )
```
